32 devices in a mesh: groups: 2 (over x), seq: 16 (over z, y, core).
Axes of the slice: x: 2, y: 2, z: 4, core: 2. Of those that a mesh axis runs over, the one named last changes fastest.
Arguments:
- queries: bfloat16 [8192, 2048], P(('groups', 'seq')), parts along dimension 0, may hold values from -14 to 14
- ctx_keys: bfloat16 [8192, 512], P(('groups', 'seq')), parts along dimension 0, may hold values from -11.5 to 11.5
- ctx_values: bfloat16 [8192, 512], P(('groups', 'seq')), parts along dimension 0, may hold values from -5 to 5
- store_keys: bfloat16 [512, 128, 512], P(('groups', 'seq')), parts along dimension 0, may hold values from -11.5 to 11.5
- store_values: bfloat16 [512, 128, 512], P(('groups', 'seq')), parts along dimension 0, may hold values from -5 to 5
- block_ids: int32 [32, 32], P(('groups', 'seq')), parts along dimension 0, may hold values from 0 to 255, as said below
- block_slot: int32 [512], P('groups'), parts along dimension 0, may hold values from 0 to 255, as said below
- gate_logit: float32 [16], replicated, may hold values from -2 to 2
Outputs:
- mixed: bfloat16 [8192, 2048], P(('groups', 'seq')), parts along dimension 0
The draws below stay inside these ranges and needn't reach their ends.
There are 2 independent parts, one for each index of `groups`. The reference program is written for one: setup_inputs(seed, part) draws one part's arguments, and reference() takes and returns one part's arrays. A program takes and returns all parts, laid end to end along the dimension named above; an argument that names none is the same for every part. Nothing has to cross between parts.
Inputs may be any that keep to these rules, and one draw needn't show every extreme that they name: block_slot is a permutation of 0 to 255; memory block b lies on seq index block_slot[b] // 16 at local position block_slot[b] % 16. `block_ids`: the 32 ids of one row are distinct; at most 2 of them lie on any one seq index, and in every draw some seq index holds exactly 2 blocks of every row.
All inputs are finite; a program needn't handle non-finite values.
Results may differ from the reference program's by a relative error of at most 0.0052.
Values may be sent and summed in bfloat16 or wider, within the bound.
A program may use at most 192 MiB of HBM per device.

```python
import jax
import jax.numpy as jnp
from jax import lax

H = 16
KVH = 4
HD = 128
QBLK = 256
MROWS = 128
TOPM = 32
CAP = 2
MEM_DEV = 16
TOKENS = 4096
NQB = 16
MEM_BLOCKS = 256


def route_tables(key):
    base = jax.random.fold_in(key, 4242)
    key_perm = jax.random.fold_in(base, 1)
    key_hot = jax.random.fold_in(base, 2)
    key_popular = jax.random.fold_in(base, 3)
    key_score = jax.random.fold_in(base, 4)
    key_first = jax.random.fold_in(base, 5)
    key_stride = jax.random.fold_in(base, 6)
    owners_count = MEM_BLOCKS // MEM_DEV
    slot_of = jax.random.permutation(key_perm, MEM_BLOCKS).astype(jnp.int32)
    id_of_slot = jnp.argsort(slot_of).astype(jnp.int32)
    hottest = jax.random.randint(key_hot, (), 0, owners_count)
    popular = jax.random.randint(key_popular, (owners_count,), 0, 2 ** 19)
    candidates = jnp.arange(owners_count * CAP, dtype=jnp.int32)
    cand_owner = candidates // CAP
    score = jax.random.randint(key_score, (NQB, owners_count * CAP), 0, 2 ** 19) + popular[cand_owner][None, :]
    score = score + jnp.where(cand_owner == hottest, 2 ** 21, 0)[None, :]
    score = score * (owners_count * CAP) + candidates[None, :]
    ignored, chosen = lax.top_k(score, TOPM)
    owner = chosen // CAP
    copy_no = chosen % CAP
    first = jax.random.randint(key_first, (NQB, owners_count), 0, MEM_DEV)
    stride = jax.random.randint(key_stride, (NQB, owners_count), 1, MEM_DEV)
    local = (jnp.take_along_axis(first, owner, axis=1) + copy_no * jnp.take_along_axis(stride, owner, axis=1)) % MEM_DEV
    slots = owner * MEM_DEV + local
    return (slot_of, id_of_slot[slots].astype(jnp.int32))


def draw_block_ids(key, part):
    return route_tables(key)[1]


def draw_block_slot(key, part):
    return route_tables(key)[0]


def draw_queries(key, part):
    inner = jax.random.fold_in(key, 11)
    field = jnp.clip(2.5 * jax.random.normal(inner, (TOKENS, H * HD), jnp.float32), -14.0, 14.0)
    return field.astype(jnp.bfloat16)


def draw_ctx_keys(key, part):
    inner = jax.random.fold_in(key, 12)
    field = jnp.clip(jax.random.normal(inner, (TOKENS, KVH * HD), jnp.float32), -4.0, 4.0)
    return field.astype(jnp.bfloat16)


def draw_store_keys(key, part):
    inner = jax.random.fold_in(key, 13)
    field = jnp.clip(jax.random.normal(inner, (MEM_BLOCKS, MROWS, KVH * HD), jnp.float32), -4.0, 4.0)
    return field.astype(jnp.bfloat16)


def block_scale(stream_key, shape, pieces, smallest, high):
    loudness, own = 1.0, jax.random.fold_in(stream_key, 6)
    for position, shards_of in pieces:
        draws = jnp.exp(jax.random.uniform(jax.random.fold_in(own, position), (shards_of,), jnp.float32, smallest / len(pieces), high / len(pieces)))
        loudness = loudness * jnp.repeat(draws, shape[position] // shards_of).reshape([-1 if axis == position else 1 for axis in range(len(shape))])
    return loudness


def normal_values(stream_key, shape, scale, limit, pieces=(), held_as=jnp.bfloat16):
    factor_of = block_scale(stream_key, shape, pieces, -0.22, 0.18) if pieces else 1.0
    array = jax.random.normal(stream_key, shape, jnp.float32) * scale * factor_of
    return jnp.minimum(jnp.maximum(array, -limit), limit).astype(held_as)


def setup_inputs(seed: int = 0, part: int = 0) -> dict:
    splits = jax.random.split(jax.random.key(seed), 9)
    part_keys = jax.random.split(jax.random.fold_in(splits[8], part), 9)
    queries = draw_queries(jax.random.fold_in(jax.random.fold_in(splits[8], part), 71), part)
    ctx_keys = draw_ctx_keys(jax.random.fold_in(jax.random.fold_in(splits[8], part), 71), part)
    ctx_values = normal_values(part_keys[2], (TOKENS, KVH * HD), 1.0, 5.0, ((0, 16),))
    store_keys = draw_store_keys(jax.random.fold_in(jax.random.fold_in(splits[8], part), 71), part)
    store_values = normal_values(part_keys[4], (MEM_BLOCKS, MROWS, KVH * HD), 1.0, 5.0, ((0, 16),))
    block_ids = draw_block_ids(jax.random.fold_in(jax.random.fold_in(splits[8], part), 71), part)
    block_slot = draw_block_slot(jax.random.fold_in(jax.random.fold_in(splits[8], part), 71), part)
    gate_logit = jnp.clip(jax.random.uniform(splits[7], (H,), jnp.float32, -2.0, 2.0), -2.0, 2.0)
    return {"queries": queries, "ctx_keys": ctx_keys, "ctx_values": ctx_values, "store_keys": store_keys, "store_values": store_values, "block_ids": block_ids, "block_slot": block_slot, "gate_logit": gate_logit}


def attend(query_rows, key_rows, value_rows, allowed):
    row_count = query_rows.shape[0]
    query_heads = query_rows.astype(jnp.float32).reshape(row_count, KVH, H // KVH, HD)
    key_heads = key_rows.astype(jnp.float32).reshape(-1, KVH, HD)
    value_heads = value_rows.astype(jnp.float32).reshape(-1, KVH, HD)
    scores = jnp.einsum("rhgd,khd->hgrk", query_heads, key_heads) * (HD ** -0.5)
    if allowed is not None:
        scores = jnp.where(allowed[None, None], scores, -1e30)
    row_max = jnp.max(scores, axis=-1, keepdims=True)
    probs = jnp.exp(scores - row_max)
    total = jnp.sum(probs, axis=-1)
    rounded = lax.optimization_barrier(probs.astype(jnp.bfloat16)).astype(jnp.float32)
    weighted = jnp.einsum("hgrk,khd->hgrd", rounded, value_heads)
    result = weighted / total[..., None]
    return jnp.transpose(result, (2, 0, 1, 3)).reshape(row_count, H * HD).astype(jnp.bfloat16)


def reference(queries, ctx_keys, ctx_values, store_keys, store_values, block_ids, block_slot, gate_logit):
    positions = jnp.arange(TOKENS, dtype=jnp.int32)
    gate = jnp.repeat(jax.nn.sigmoid(gate_logit.astype(jnp.float32)), HD)

    def one_block(block_no):
        start = (block_no * QBLK).astype(jnp.int32)
        query_rows = lax.dynamic_slice_in_dim(queries, start, QBLK, 0)
        query_pos = start + jnp.arange(QBLK, dtype=jnp.int32)
        allowed = positions[None, :] <= query_pos[:, None]
        context = attend(query_rows, ctx_keys, ctx_values, allowed)
        slots = block_slot[block_ids[block_no]]
        memory_keys = store_keys[slots].reshape(TOPM * MROWS, KVH * HD)
        memory_values = store_values[slots].reshape(TOPM * MROWS, KVH * HD)
        memory = attend(query_rows, memory_keys, memory_values, None)
        memory_wide = lax.optimization_barrier(memory).astype(jnp.float32)
        context_wide = lax.optimization_barrier(context).astype(jnp.float32)
        return (gate * memory_wide + (1.0 - gate) * context_wide).astype(jnp.bfloat16)

    blocks = lax.map(one_block, jnp.arange(NQB, dtype=jnp.int32))
    return blocks.reshape(TOKENS, H * HD)
```

```python
import functools

import jax
import jax.numpy as jnp
from jax import lax
from jax.experimental import pallas as pl
from jax.experimental.pallas import tpu as pltpu
from jax.sharding import PartitionSpec as P

H = 16
KVH = 4
HD = 128
GROUP = H // KVH
QBLK = 256
MROWS = 128
TOPM = 32
CAP = 2
SLAB = CAP * MROWS
TILE = 1024
SRCS = TILE // SLAB

NEG = -1e30
SCALE2 = HD ** (-0.5) * 1.4426950408889634
VMEM_LIMIT = 60 * 1024 * 1024


def request_table(slots, owners_count, capacity, local_count):
    entries = slots.shape[0]
    owner = slots // local_count
    local = slots % local_count
    order = jnp.arange(entries, dtype=jnp.int32)
    earlier = (owner[:, None] == owner[None, :]) & (order[None, :] < order[:, None])
    rank = jnp.sum(earlier.astype(jnp.int32), axis=1)
    chosen = (owner[:, None, None] == jnp.arange(owners_count, dtype=jnp.int32)[None, :, None]) & (
        rank[:, None, None] == jnp.arange(capacity, dtype=jnp.int32)[None, None, :]
    )
    return jnp.sum(jnp.where(chosen, local[:, None, None] + 1, 0), axis=0) - 1


def lookup_slots(wanted_ids, block_slot):
    hits = wanted_ids[..., None] == jnp.arange(block_slot.shape[0], dtype=jnp.int32)
    return jnp.sum(jnp.where(hits, block_slot, 0), axis=-1)


def fresh(rows):
    return (
        jnp.full((rows, 1), NEG, jnp.float32),
        jnp.zeros((rows, 1), jnp.float32),
        jnp.zeros((rows, HD), jnp.float32),
    )


def tile_update(state, q, k, v, bias=None, allowed=None):
    m, l, acc = state
    s = lax.dot_general(q, k, (((1,), (1,)), ((), ())), preferred_element_type=jnp.float32)
    s = s * SCALE2
    if bias is not None:
        s = s + bias
    if allowed is not None:
        s = jnp.where(allowed, s, NEG)
    m_new = jnp.maximum(m, jnp.max(s, axis=-1, keepdims=True))
    decay = jnp.exp2(m - m_new)
    p = jnp.exp2(s - m_new)
    l = l * decay + jnp.sum(p, axis=-1, keepdims=True)
    acc = acc * decay + jnp.dot(p.astype(jnp.bfloat16), v, preferred_element_type=jnp.float32)
    return (m_new, l, acc)


def lanes_of(j):
    return pl.ds(pl.multiple_of(j * HD, HD), HD)


def memory_kernel(size, masked, *refs):
    if masked:
        q_ref, sk_ref, sv_ref, bias_ref = refs[:4]
        refs = refs[4:]
    else:
        q_ref, sk_ref, sv_ref = refs[:3]
        bias_ref = None
        refs = refs[3:]
    (out_ref, qp, rk, rv, po, ps, ro, rs, q_sem, send_sem, recv_sem, self_sem, res_sem, st_sem) = refs
    half_size = size // 2
    me = lax.axis_index("seq")
    mine = me // half_size
    spot = me % half_size
    partner = (me + half_size) % size
    rows = q_ref.shape[0]

    barrier = pltpu.get_barrier_semaphore()

    def greet(step, carry):
        peer = mine * half_size + (spot + step) % half_size
        pl.semaphore_signal(barrier, inc=1, device_id={"seq": peer}, device_id_type=pl.DeviceIdType.MESH)
        return carry

    lax.fori_loop(1, half_size, greet, 0)
    pl.semaphore_signal(barrier, inc=1, device_id={"seq": partner}, device_id_type=pl.DeviceIdType.MESH)
    pl.semaphore_wait(barrier, half_size)

    def query_copy():
        return pltpu.make_async_remote_copy(
            src_ref=q_ref, dst_ref=qp, send_sem=q_sem.at[0], recv_sem=q_sem.at[1],
            device_id={"seq": partner}, device_id_type=pl.DeviceIdType.MESH,
        )

    def self_copies(kind):
        asker = me if kind == 0 else partner
        return (
            pltpu.make_async_copy(sk_ref.at[asker], rk.at[kind, spot], self_sem.at[kind, 0]),
            pltpu.make_async_copy(sv_ref.at[asker], rv.at[kind, spot], self_sem.at[kind, 1]),
        )

    def slab_copies(kind, step):
        peer_spot = (spot + step) % half_size
        peer = mine * half_size + peer_spot
        asker = peer if kind == 0 else (1 - mine) * half_size + peer_spot
        return tuple(
            pltpu.make_async_remote_copy(
                src_ref=src.at[asker], dst_ref=dst.at[kind, spot],
                send_sem=send_sem.at[kind, which, step], recv_sem=recv_sem.at[kind, which, spot],
                device_id={"seq": peer}, device_id_type=pl.DeviceIdType.MESH,
            )
            for which, (src, dst) in enumerate(((sk_ref, rk), (sv_ref, rv)))
        )

    def slab_arrivals(kind, step):
        from_spot = (spot + step) % half_size
        return tuple(
            pltpu.make_async_remote_copy(
                src_ref=src.at[0], dst_ref=dst.at[kind, from_spot],
                send_sem=send_sem.at[kind, which, step], recv_sem=recv_sem.at[kind, which, from_spot],
                device_id={"seq": partner}, device_id_type=pl.DeviceIdType.MESH,
            )
            for which, (src, dst) in enumerate(((sk_ref, rk), (sv_ref, rv)))
        )

    def send_all(kind):
        def send(step, carry):
            for copy in slab_copies(kind, step):
                copy.start()
            return carry

        for copy in self_copies(kind):
            copy.start()
        lax.fori_loop(1, half_size, send, 0)

    def receive_all(kind):
        def receive(step, carry):
            for copy in slab_arrivals(kind, step):
                copy.wait_recv()
            return carry

        for copy in self_copies(kind):
            copy.wait()
        lax.fori_loop(1, half_size, receive, 0)

    def result_copy(g):
        part = pl.ds(pl.multiple_of(g * GROUP * HD, GROUP * HD), GROUP * HD)
        return pltpu.make_async_remote_copy(
            src_ref=po.at[:, part], dst_ref=ro.at[:, part],
            send_sem=res_sem.at[0, g], recv_sem=res_sem.at[1, g],
            device_id={"seq": partner}, device_id_type=pl.DeviceIdType.MESH,
        )

    def stats_copy():
        return pltpu.make_async_remote_copy(
            src_ref=ps, dst_ref=rs, send_sem=st_sem.at[0], recv_sem=st_sem.at[1],
            device_id={"seq": partner}, device_id_type=pl.DeviceIdType.MESH,
        )

    def head_state(kind, source, j):
        q = source[:, lanes_of(j)]
        kv = lanes_of(j // GROUP)
        state = fresh(rows)
        for t in range(half_size // SRCS):
            k = rk[kind, t * SRCS:(t + 1) * SRCS, :, kv].reshape(TILE, HD)
            v = rv[kind, t * SRCS:(t + 1) * SRCS, :, kv].reshape(TILE, HD)
            bias = None if bias_ref is None else bias_ref[kind, :, t * TILE:(t + 1) * TILE]
            state = tile_update(state, q, k, v, bias=bias)
        return state

    lane = lax.broadcasted_iota(jnp.int32, (rows, HD), 1)

    query_copy().start()
    send_all(1)
    send_all(0)
    query_copy().wait_recv()
    receive_all(1)

    stats = jnp.zeros((rows, HD), jnp.float32)
    for g in range(KVH):

        def serve(i, st, g=g):
            j = g * GROUP + i
            m, l, acc = head_state(1, qp, j)
            po[:, lanes_of(j)] = (acc / l).astype(jnp.bfloat16)
            st = jnp.where(lane == j, m, st)
            return jnp.where(lane == j + H, l, st)

        stats = lax.fori_loop(0, GROUP, serve, stats)
        if g == KVH - 1:
            ps[...] = stats
        else:
            if g >= 1:
                result_copy(g - 1).start()
    receive_all(0)
    result_copy(KVH - 2).start()
    result_copy(KVH - 1).start()
    stats_copy().start()

    def merge(j, state):
        m, l, acc = state
        there = rs[...]
        m_far = jnp.sum(jnp.where(lane == j, there, 0.0), axis=-1, keepdims=True)
        l_far = jnp.sum(jnp.where(lane == j + H, there, 0.0), axis=-1, keepdims=True)
        top = jnp.maximum(m, m_far)
        w = jnp.exp2(m - top)
        w_far = jnp.exp2(m_far - top) * l_far
        far = ro[:, lanes_of(j)].astype(jnp.float32)
        out_ref[:, lanes_of(j)] = ((acc * w + far * w_far) / (l * w + w_far)).astype(jnp.bfloat16)

    stats_copy().wait_recv()
    for g in range(KVH):
        result_copy(g).wait_recv()

        def finish(i, carry, g=g):
            j = g * GROUP + i
            merge(j, head_state(0, q_ref, j))
            return carry

        lax.fori_loop(0, GROUP, finish, 0)

    query_copy().wait_send()
    for kind in (1, 0):

        def drain(step, carry, kind=kind):
            for copy in slab_copies(kind, step):
                copy.wait_send()
            return carry

        lax.fori_loop(1, half_size, drain, 0)
    for g in range(KVH):
        result_copy(g).wait_send()
    stats_copy().wait_send()


def memory_call(queries, send_keys, send_values, bias, size):
    rows = queries.shape[0]
    half_size = size // 2
    operands = [queries, send_keys, send_values]
    specs = [
        pl.BlockSpec(memory_space=pltpu.VMEM),
        pl.BlockSpec(memory_space=pl.ANY),
        pl.BlockSpec(memory_space=pl.ANY),
    ]
    if bias is not None:
        operands.append(bias)
        specs.append(pl.BlockSpec(memory_space=pltpu.VMEM))
    width = KVH * HD
    return pl.pallas_call(
        functools.partial(memory_kernel, size, bias is not None),
        out_shape=jax.ShapeDtypeStruct(queries.shape, jnp.bfloat16),
        in_specs=specs,
        out_specs=pl.BlockSpec(memory_space=pltpu.VMEM),
        scratch_shapes=[
            pltpu.VMEM(queries.shape, jnp.bfloat16),
            pltpu.VMEM((2, half_size, SLAB, width), jnp.bfloat16),
            pltpu.VMEM((2, half_size, SLAB, width), jnp.bfloat16),
            pltpu.VMEM(queries.shape, jnp.bfloat16),
            pltpu.VMEM((rows, HD), jnp.float32),
            pltpu.VMEM(queries.shape, jnp.bfloat16),
            pltpu.VMEM((rows, HD), jnp.float32),
            pltpu.SemaphoreType.DMA((2,)),
            pltpu.SemaphoreType.DMA((2, 2, half_size)),
            pltpu.SemaphoreType.DMA((2, 2, half_size)),
            pltpu.SemaphoreType.DMA((2, 2)),
            pltpu.SemaphoreType.DMA((2, KVH)),
            pltpu.SemaphoreType.DMA((2,)),
        ],
        compiler_params=pltpu.CompilerParams(
            collective_id=0, has_side_effects=True, vmem_limit_bytes=VMEM_LIMIT
        ),
        cost_estimate=pl.CostEstimate(
            flops=16 * 4096 * 256 * 512, bytes_accessed=200_000_000, transcendentals=16 * 4096 * 256
        ),
    )(*operands)


def context_kernel(gate_ref, pos_ref, q_ref, k_ref, v_ref, mem_ref, out_ref):
    rows = q_ref.shape[0]
    start = pos_ref[0]
    last = start // TILE
    spots = start + lax.broadcasted_iota(jnp.int32, (rows, TILE), 0)
    keys = last * TILE + lax.broadcasted_iota(jnp.int32, (rows, TILE), 1)
    allowed = keys <= spots

    def head(j, carry):
        q = q_ref[:, lanes_of(j)]
        kv = lanes_of(j // GROUP)

        def piece(t):
            at = pl.ds(pl.multiple_of(t * TILE, TILE), TILE)
            return k_ref[at, kv], v_ref[at, kv]

        k, v = piece(last)
        state = tile_update(fresh(rows), q, k, v, allowed=allowed)

        def step(t, state):
            k, v = piece(t)
            return tile_update(state, q, k, v)

        m, l, acc = lax.fori_loop(0, last, step, state)
        context = (acc / l).astype(jnp.bfloat16).astype(jnp.float32)
        memory = mem_ref[:, lanes_of(j)].astype(jnp.float32)
        g = gate_ref[j]
        out_ref[:, lanes_of(j)] = (g * memory + (1.0 - g) * context).astype(jnp.bfloat16)
        return carry

    lax.fori_loop(0, H, head, 0)


def context_call(gate, start, queries, keys, values, memory):
    full = pl.BlockSpec(memory_space=pltpu.VMEM)
    scalar = pl.BlockSpec(memory_space=pltpu.SMEM)
    return pl.pallas_call(
        context_kernel,
        out_shape=jax.ShapeDtypeStruct(queries.shape, jnp.bfloat16),
        in_specs=[scalar, scalar, full, full, full, full],
        out_specs=full,
        compiler_params=pltpu.CompilerParams(vmem_limit_bytes=VMEM_LIMIT),
    )(gate, start, queries, keys, values, memory)


def on_device(
    queries, ctx_keys, ctx_values, store_keys, store_values, block_ids, block_slot, gate_logit
):
    size = lax.axis_size("seq")
    half_size = size // 2
    me = lax.axis_index("seq")
    local_count = store_keys.shape[0]
    my_slots = lookup_slots(block_ids.reshape(-1), block_slot)
    my_table = request_table(my_slots, size, CAP, local_count)
    wanted = lax.all_to_all(my_table, "seq", split_axis=0, concat_axis=0, tiled=True)
    rows_wanted = jnp.maximum(wanted, 0)
    width = KVH * HD
    send_keys = store_keys[rows_wanted].reshape(size, SLAB, width)
    send_values = store_values[rows_wanted].reshape(size, SLAB, width)
    bias = None
    if size * CAP != TOPM:
        tables = lax.all_gather(my_table, "seq", axis=0)
        half_start = me // half_size * half_size
        two = jnp.stack([tables[me], tables[(me + half_size) % size]])
        two = lax.dynamic_slice_in_dim(two, half_start, half_size, 1).reshape(2, half_size * CAP)
        bias = jnp.repeat(jnp.where(two < 0, NEG, 0.0).astype(jnp.float32), MROWS, axis=1)[:, None, :]
    key_all = lax.all_gather(ctx_keys, "seq", axis=0, tiled=True)
    value_all = lax.all_gather(ctx_values, "seq", axis=0, tiled=True)
    memory = memory_call(queries, send_keys, send_values, bias, size)
    gate = jax.nn.sigmoid(gate_logit)
    start = jnp.reshape(me * queries.shape[0], (1,)).astype(jnp.int32)
    return context_call(gate, start, queries, key_all, value_all, memory)


def solution(mesh):
    placed = (
        P(("groups", "seq"), None),
        P(("groups", "seq"), None),
        P(("groups", "seq"), None),
        P(("groups", "seq"), None, None),
        P(("groups", "seq"), None, None),
        P(("groups", "seq"), None),
        P("groups"),
        P(),
    )
    return jax.shard_map(
        on_device, mesh=mesh, in_specs=placed, out_specs=P(("groups", "seq"), None), check_vma=False
    )
```

```python
import functools

import jax
import jax.numpy as jnp
from jax import lax
from jax.experimental import pallas as pl
from jax.experimental.pallas import tpu as pltpu
from jax.sharding import PartitionSpec as P

H = 16
KVH = 4
HD = 128
GROUP = H // KVH
QBLK = 256
MROWS = 128
TOPM = 32
CAP = 2
SLAB = CAP * MROWS
TILE = 1024
SRCS = TILE // SLAB
PLANE = 4

NEG = -1e30
SCALE2 = HD ** (-0.5) * 1.4426950408889634
VMEM_LIMIT = 60 * 1024 * 1024


def request_table(slots, owners_count, capacity, local_count):
    entries = slots.shape[0]
    owner = slots // local_count
    local = slots % local_count
    order = jnp.arange(entries, dtype=jnp.int32)
    earlier = (owner[:, None] == owner[None, :]) & (order[None, :] < order[:, None])
    rank = jnp.sum(earlier.astype(jnp.int32), axis=1)
    chosen = (owner[:, None, None] == jnp.arange(owners_count, dtype=jnp.int32)[None, :, None]) & (
        rank[:, None, None] == jnp.arange(capacity, dtype=jnp.int32)[None, None, :]
    )
    return jnp.sum(jnp.where(chosen, local[:, None, None] + 1, 0), axis=0) - 1


def lookup_slots(wanted_ids, block_slot):
    hits = wanted_ids[..., None] == jnp.arange(block_slot.shape[0], dtype=jnp.int32)
    return jnp.sum(jnp.where(hits, block_slot, 0), axis=-1)


def fresh(rows):
    return (
        jnp.full((rows, 1), NEG, jnp.float32),
        jnp.zeros((rows, 1), jnp.float32),
        jnp.zeros((rows, HD), jnp.float32),
    )


def tile_update(state, q, k, v, bias=None, allowed=None):
    m, l, acc = state
    s = lax.dot_general(q, k, (((1,), (1,)), ((), ())), preferred_element_type=jnp.float32)
    s = s * SCALE2
    if bias is not None:
        s = s + bias
    if allowed is not None:
        s = jnp.where(allowed, s, NEG)
    m_new = jnp.maximum(m, jnp.max(s, axis=-1, keepdims=True))
    decay = jnp.exp2(m - m_new)
    p = jnp.exp2(s - m_new)
    l = l * decay + jnp.sum(p, axis=-1, keepdims=True)
    acc = acc * decay + jnp.dot(p.astype(jnp.bfloat16), v, preferred_element_type=jnp.float32)
    return (m_new, l, acc)


def lanes_of(j):
    return pl.ds(pl.multiple_of(j * HD, HD), HD)


def attention_kernel(size, masked, *refs):
    if masked:
        gate_ref, q_ref, key_ref, value_ref, sk_ref, sv_ref, bias_ref = refs[:7]
        refs = refs[7:]
    else:
        gate_ref, q_ref, key_ref, value_ref, sk_ref, sv_ref = refs[:6]
        bias_ref = None
        refs = refs[6:]
    (out_ref, qp, rk, rv, po, ps, ro, rs, ck, cv, q_sem, send_sem, recv_sem, self_sem, res_sem, st_sem,
     own_sem, up_sem, side_sem, core_sem) = refs
    half_size = size // 2
    me = lax.axis_index("seq")
    mine = me // half_size
    spot = me % half_size
    partner = (me + half_size) % size
    rows = q_ref.shape[0]
    planes = size // PLANE
    plane = me // PLANE
    side = me % PLANE // 2
    core = me % 2
    above = (me + PLANE) % size

    own_copies = (
        pltpu.make_async_copy(key_ref, ck.at[me], own_sem.at[0]),
        pltpu.make_async_copy(value_ref, cv.at[me], own_sem.at[1]),
    )
    for copy in own_copies:
        copy.start()

    barrier = pltpu.get_barrier_semaphore()

    def greet(step, carry):
        peer = mine * half_size + (spot + step) % half_size
        pl.semaphore_signal(barrier, inc=1, device_id={"seq": peer}, device_id_type=pl.DeviceIdType.MESH)
        return carry

    lax.fori_loop(1, half_size, greet, 0)
    pl.semaphore_signal(barrier, inc=1, device_id={"seq": partner}, device_id_type=pl.DeviceIdType.MESH)
    for near in ((me + PLANE) % size, (me + size - PLANE) % size):
        pl.semaphore_signal(barrier, inc=1, device_id={"seq": near}, device_id_type=pl.DeviceIdType.MESH)
    pl.semaphore_wait(barrier, half_size + 2)

    def chunk_copies(chunk, peer, send, recv):
        return tuple(
            pltpu.make_async_remote_copy(
                src_ref=buf.at[chunk], dst_ref=buf.at[chunk],
                send_sem=send(which), recv_sem=recv(which),
                device_id={"seq": peer}, device_id_type=pl.DeviceIdType.MESH,
            )
            for which, buf in enumerate((ck, cv))
        )

    def up_copies(p):
        return chunk_copies(
            p * PLANE + me % PLANE, above, lambda w: up_sem.at[0, w, p], lambda w: up_sem.at[1, w, p]
        )

    def side_copies(p, y):
        return chunk_copies(
            p * PLANE + y * 2 + core, plane * PLANE + (1 - side) * 2 + core,
            lambda w: side_sem.at[0, w, p], lambda w: side_sem.at[1, w, p],
        )

    def core_copies(p, y, c):
        return chunk_copies(
            p * PLANE + y * 2 + c, plane * PLANE + side * 2 + (1 - core),
            lambda w: core_sem.at[0, w, p, y], lambda w: core_sem.at[1, w, p, y],
        )

    def start(copies):
        for copy in copies:
            copy.start()

    def arrive(copies):
        for copy in copies:
            copy.wait_recv()

    def left(copies):
        for copy in copies:
            copy.wait_send()

    def pass_on(p):
        @pl.when(plane < planes - 1)
        def _():
            start(up_copies(p))

        start(side_copies(p, side))
        start(core_copies(p, side, core))

    def pass_side(p):
        arrive(side_copies(p, 1 - side))
        start(core_copies(p, 1 - side, core))

    def query_copy():
        return pltpu.make_async_remote_copy(
            src_ref=q_ref, dst_ref=qp, send_sem=q_sem.at[0], recv_sem=q_sem.at[1],
            device_id={"seq": partner}, device_id_type=pl.DeviceIdType.MESH,
        )

    def self_copies(kind):
        asker = me if kind == 0 else partner
        return (
            pltpu.make_async_copy(sk_ref.at[asker], rk.at[kind, spot], self_sem.at[kind, 0]),
            pltpu.make_async_copy(sv_ref.at[asker], rv.at[kind, spot], self_sem.at[kind, 1]),
        )

    def slab_copies(kind, step):
        peer_spot = (spot + step) % half_size
        peer = mine * half_size + peer_spot
        asker = peer if kind == 0 else (1 - mine) * half_size + peer_spot
        return tuple(
            pltpu.make_async_remote_copy(
                src_ref=src.at[asker], dst_ref=dst.at[kind, spot],
                send_sem=send_sem.at[kind, which, step], recv_sem=recv_sem.at[kind, which, spot],
                device_id={"seq": peer}, device_id_type=pl.DeviceIdType.MESH,
            )
            for which, (src, dst) in enumerate(((sk_ref, rk), (sv_ref, rv)))
        )

    def slab_arrivals(kind, step):
        from_spot = (spot + step) % half_size
        return tuple(
            pltpu.make_async_remote_copy(
                src_ref=src.at[0], dst_ref=dst.at[kind, from_spot],
                send_sem=send_sem.at[kind, which, step], recv_sem=recv_sem.at[kind, which, from_spot],
                device_id={"seq": partner}, device_id_type=pl.DeviceIdType.MESH,
            )
            for which, (src, dst) in enumerate(((sk_ref, rk), (sv_ref, rv)))
        )

    def send_all(kind):
        def send(step, carry):
            for copy in slab_copies(kind, step):
                copy.start()
            return carry

        for copy in self_copies(kind):
            copy.start()
        lax.fori_loop(1, half_size, send, 0)

    def receive_all(kind):
        def receive(step, carry):
            for copy in slab_arrivals(kind, step):
                copy.wait_recv()
            return carry

        for copy in self_copies(kind):
            copy.wait()
        lax.fori_loop(1, half_size, receive, 0)

    def result_copy(g):
        part = pl.ds(pl.multiple_of(g * GROUP * HD, GROUP * HD), GROUP * HD)
        return pltpu.make_async_remote_copy(
            src_ref=po.at[:, part], dst_ref=ro.at[:, part],
            send_sem=res_sem.at[0, g], recv_sem=res_sem.at[1, g],
            device_id={"seq": partner}, device_id_type=pl.DeviceIdType.MESH,
        )

    def stats_copy():
        return pltpu.make_async_remote_copy(
            src_ref=ps, dst_ref=rs, send_sem=st_sem.at[0], recv_sem=st_sem.at[1],
            device_id={"seq": partner}, device_id_type=pl.DeviceIdType.MESH,
        )

    def head_state(kind, source, j):
        q = source[:, lanes_of(j)]
        kv = lanes_of(j // GROUP)
        state = fresh(rows)
        for t in range(half_size // SRCS):
            k = rk[kind, t * SRCS:(t + 1) * SRCS, :, kv].reshape(TILE, HD)
            v = rv[kind, t * SRCS:(t + 1) * SRCS, :, kv].reshape(TILE, HD)
            bias = None if bias_ref is None else bias_ref[kind, :, t * TILE:(t + 1) * TILE]
            state = tile_update(state, q, k, v, bias=bias)
        return state

    lane = lax.broadcasted_iota(jnp.int32, (rows, HD), 1)

    for copy in own_copies:
        copy.wait()
    pass_on(plane)
    query_copy().start()
    send_all(1)

    def relay(t, carry):
        arrive(up_copies(plane - t))
        pass_on(plane - t)
        pass_side(plane - t + 1)
        return carry

    lax.fori_loop(1, plane + 1, relay, 0)
    pass_side(0)
    send_all(0)
    query_copy().wait_recv()
    receive_all(1)

    stats = jnp.zeros((rows, HD), jnp.float32)
    for g in range(KVH):

        def serve(i, st, g=g):
            j = g * GROUP + i
            m, l, acc = head_state(1, qp, j)
            po[:, lanes_of(j)] = (acc / l).astype(jnp.bfloat16)
            st = jnp.where(lane == j, m, st)
            return jnp.where(lane == j + H, l, st)

        stats = lax.fori_loop(0, GROUP, serve, stats)
        if g == KVH - 1:
            ps[...] = stats
        else:
            if g >= 1:
                result_copy(g - 1).start()
    result_copy(KVH - 2).start()

    def core_arrivals(t, carry):
        arrive(core_copies(t, side, 1 - core))
        arrive(core_copies(t, 1 - side, 1 - core))
        return carry

    lax.fori_loop(0, plane + 1, core_arrivals, 0)
    result_copy(KVH - 1).start()
    stats_copy().start()

    spots = me % PLANE * rows + lax.broadcasted_iota(jnp.int32, (rows, TILE), 0)
    allowed = lax.broadcasted_iota(jnp.int32, (rows, TILE), 1) <= spots

    def context_head(j, carry):
        q = q_ref[:, lanes_of(j)]
        kv = lanes_of(j // GROUP)

        def piece(t):
            at = pl.ds(t * PLANE, PLANE)
            return ck[at, :, kv].reshape(TILE, HD), cv[at, :, kv].reshape(TILE, HD)

        k, v = piece(plane)
        state = tile_update(fresh(rows), q, k, v, allowed=allowed)

        def step(t, state):
            k, v = piece(t)
            return tile_update(state, q, k, v)

        m, l, acc = lax.fori_loop(0, plane, step, state)
        out_ref[:, lanes_of(j)] = (acc / l).astype(jnp.bfloat16)
        return carry

    lax.fori_loop(0, H, context_head, 0)
    receive_all(0)

    def merge(j, state):
        m, l, acc = state
        there = rs[...]
        m_far = jnp.sum(jnp.where(lane == j, there, 0.0), axis=-1, keepdims=True)
        l_far = jnp.sum(jnp.where(lane == j + H, there, 0.0), axis=-1, keepdims=True)
        top = jnp.maximum(m, m_far)
        w = jnp.exp2(m - top)
        w_far = jnp.exp2(m_far - top) * l_far
        far = ro[:, lanes_of(j)].astype(jnp.float32)
        memory = ((acc * w + far * w_far) / (l * w + w_far)).astype(jnp.bfloat16).astype(jnp.float32)
        context = out_ref[:, lanes_of(j)].astype(jnp.float32)
        gate = gate_ref[j]
        out_ref[:, lanes_of(j)] = (gate * memory + (1.0 - gate) * context).astype(jnp.bfloat16)

    stats_copy().wait_recv()
    for g in range(KVH):
        result_copy(g).wait_recv()

        def finish(i, carry, g=g):
            j = g * GROUP + i
            merge(j, head_state(0, q_ref, j))
            return carry

        lax.fori_loop(0, GROUP, finish, 0)

    def drain_context(p, carry):
        @pl.when(plane < planes - 1)
        def _():
            left(up_copies(p))

        left(side_copies(p, side))
        left(core_copies(p, side, core))
        left(core_copies(p, 1 - side, core))
        return carry

    lax.fori_loop(0, plane + 1, drain_context, 0)
    query_copy().wait_send()
    for kind in (1, 0):

        def drain(step, carry, kind=kind):
            for copy in slab_copies(kind, step):
                copy.wait_send()
            return carry

        lax.fori_loop(1, half_size, drain, 0)
    for g in range(KVH):
        result_copy(g).wait_send()
    stats_copy().wait_send()


def attention_call(gate, queries, keys, values, send_keys, send_values, bias, size):
    rows = queries.shape[0]
    half_size = size // 2
    planes = size // PLANE
    operands = [gate, queries, keys, values, send_keys, send_values]
    specs = [
        pl.BlockSpec(memory_space=pltpu.SMEM),
        pl.BlockSpec(memory_space=pltpu.VMEM),
        pl.BlockSpec(memory_space=pl.ANY),
        pl.BlockSpec(memory_space=pl.ANY),
        pl.BlockSpec(memory_space=pl.ANY),
        pl.BlockSpec(memory_space=pl.ANY),
    ]
    if bias is not None:
        operands.append(bias)
        specs.append(pl.BlockSpec(memory_space=pltpu.VMEM))
    width = KVH * HD
    return pl.pallas_call(
        functools.partial(attention_kernel, size, bias is not None),
        out_shape=jax.ShapeDtypeStruct(queries.shape, jnp.bfloat16),
        in_specs=specs,
        out_specs=pl.BlockSpec(memory_space=pltpu.VMEM),
        scratch_shapes=[
            pltpu.VMEM(queries.shape, jnp.bfloat16),
            pltpu.VMEM((2, half_size, SLAB, width), jnp.bfloat16),
            pltpu.VMEM((2, half_size, SLAB, width), jnp.bfloat16),
            pltpu.VMEM(queries.shape, jnp.bfloat16),
            pltpu.VMEM((rows, HD), jnp.float32),
            pltpu.VMEM(queries.shape, jnp.bfloat16),
            pltpu.VMEM((rows, HD), jnp.float32),
            pltpu.VMEM((size, rows, width), jnp.bfloat16),
            pltpu.VMEM((size, rows, width), jnp.bfloat16),
            pltpu.SemaphoreType.DMA((2,)),
            pltpu.SemaphoreType.DMA((2, 2, half_size)),
            pltpu.SemaphoreType.DMA((2, 2, half_size)),
            pltpu.SemaphoreType.DMA((2, 2)),
            pltpu.SemaphoreType.DMA((2, KVH)),
            pltpu.SemaphoreType.DMA((2,)),
            pltpu.SemaphoreType.DMA((2,)),
            pltpu.SemaphoreType.DMA((2, 2, planes)),
            pltpu.SemaphoreType.DMA((2, 2, planes)),
            pltpu.SemaphoreType.DMA((2, 2, planes, 2)),
        ],
        compiler_params=pltpu.CompilerParams(
            collective_id=0, has_side_effects=True, vmem_limit_bytes=VMEM_LIMIT
        ),
        cost_estimate=pl.CostEstimate(
            flops=16 * 4096 * 256 * 512, bytes_accessed=200_000_000, transcendentals=16 * 4096 * 256
        ),
    )(*operands)


def on_device(
    queries, ctx_keys, ctx_values, store_keys, store_values, block_ids, block_slot, gate_logit
):
    size = lax.axis_size("seq")
    half_size = size // 2
    me = lax.axis_index("seq")
    local_count = store_keys.shape[0]
    my_slots = lookup_slots(block_ids.reshape(-1), block_slot)
    my_table = request_table(my_slots, size, CAP, local_count)
    wanted = lax.all_to_all(my_table, "seq", split_axis=0, concat_axis=0, tiled=True)
    rows_wanted = jnp.maximum(wanted, 0)
    width = KVH * HD
    send_keys = store_keys[rows_wanted].reshape(size, SLAB, width)
    send_values = store_values[rows_wanted].reshape(size, SLAB, width)
    bias = None
    if size * CAP != TOPM:
        tables = lax.all_gather(my_table, "seq", axis=0)
        half_start = me // half_size * half_size
        two = jnp.stack([tables[me], tables[(me + half_size) % size]])
        two = lax.dynamic_slice_in_dim(two, half_start, half_size, 1).reshape(2, half_size * CAP)
        bias = jnp.repeat(jnp.where(two < 0, NEG, 0.0).astype(jnp.float32), MROWS, axis=1)[:, None, :]
    gate = jax.nn.sigmoid(gate_logit)
    return attention_call(gate, queries, ctx_keys, ctx_values, send_keys, send_values, bias, size)


def solution(mesh):
    placed = (
        P(("groups", "seq"), None),
        P(("groups", "seq"), None),
        P(("groups", "seq"), None),
        P(("groups", "seq"), None, None),
        P(("groups", "seq"), None, None),
        P(("groups", "seq"), None),
        P("groups"),
        P(),
    )
    return jax.shard_map(
        on_device, mesh=mesh, in_specs=placed, out_specs=P(("groups", "seq"), None), check_vma=False
    )
```

```python
import functools

import jax
import jax.numpy as jnp
from jax import lax
from jax.experimental import pallas as pl
from jax.experimental.pallas import tpu as pltpu
from jax.sharding import PartitionSpec as P

H = 16
KVH = 4
HD = 128
GROUP = H // KVH
QBLK = 256
MROWS = 128
TOPM = 32
CAP = 2
SLAB = CAP * MROWS
TILE = 1024
SRCS = TILE // SLAB
PLANE = 4

NEG = -1e30
SCALE2 = HD ** (-0.5) * 1.4426950408889634
VMEM_LIMIT = 60 * 1024 * 1024


def request_table(slots, owners_count, capacity, local_count):
    entries = slots.shape[0]
    owner = slots // local_count
    local = slots % local_count
    order = jnp.arange(entries, dtype=jnp.int32)
    earlier = (owner[:, None] == owner[None, :]) & (order[None, :] < order[:, None])
    rank = jnp.sum(earlier.astype(jnp.int32), axis=1)
    chosen = (owner[:, None, None] == jnp.arange(owners_count, dtype=jnp.int32)[None, :, None]) & (
        rank[:, None, None] == jnp.arange(capacity, dtype=jnp.int32)[None, None, :]
    )
    return jnp.sum(jnp.where(chosen, local[:, None, None] + 1, 0), axis=0) - 1


def lookup_slots(wanted_ids, block_slot):
    hits = wanted_ids[..., None] == jnp.arange(block_slot.shape[0], dtype=jnp.int32)
    return jnp.sum(jnp.where(hits, block_slot, 0), axis=-1)


def fresh(rows):
    return (
        jnp.full((rows, 1), NEG, jnp.float32),
        jnp.zeros((rows, 1), jnp.float32),
        jnp.zeros((rows, HD), jnp.float32),
    )


def tile_update(state, q, k, v, bias=None, allowed=None):
    m, l, acc = state
    s = lax.dot_general(q, k, (((1,), (1,)), ((), ())), preferred_element_type=jnp.float32)
    s = s * SCALE2
    if bias is not None:
        s = s + bias
    if allowed is not None:
        s = jnp.where(allowed, s, NEG)
    m_new = jnp.maximum(m, jnp.max(s, axis=-1, keepdims=True))
    decay = jnp.exp2(m - m_new)
    p = jnp.exp2(s - m_new)
    l = l * decay + jnp.sum(p, axis=-1, keepdims=True)
    acc = acc * decay + jnp.dot(p.astype(jnp.bfloat16), v, preferred_element_type=jnp.float32)
    return (m_new, l, acc)


def lanes_of(j):
    return pl.ds(pl.multiple_of(j * HD, HD), HD)


def attention_kernel(size, masked, *refs):
    if masked:
        gate_ref, q_ref, key_ref, value_ref, sk_ref, sv_ref, bias_ref = refs[:7]
        refs = refs[7:]
    else:
        gate_ref, q_ref, key_ref, value_ref, sk_ref, sv_ref = refs[:6]
        bias_ref = None
        refs = refs[6:]
    (out_ref, qp, rk, rv, po, ps, ro, rs, ck, cv, q_sem, send_sem, recv_sem, self_sem, res_sem, st_sem,
     own_sem, up_sem, side_sem, core_sem) = refs
    half_size = size // 2
    me = lax.axis_index("seq")
    mine = me // half_size
    spot = me % half_size
    partner = (me + half_size) % size
    rows = q_ref.shape[0]
    planes = size // PLANE
    plane = me // PLANE
    side = me % PLANE // 2
    core = me % 2
    above = (me + PLANE) % size

    own_copies = (
        pltpu.make_async_copy(key_ref, ck.at[me], own_sem.at[0]),
        pltpu.make_async_copy(value_ref, cv.at[me], own_sem.at[1]),
    )
    for copy in own_copies:
        copy.start()

    barrier = pltpu.get_barrier_semaphore()

    def greet(step, carry):
        peer = mine * half_size + (spot + step) % half_size
        pl.semaphore_signal(barrier, inc=1, device_id={"seq": peer}, device_id_type=pl.DeviceIdType.MESH)
        return carry

    lax.fori_loop(1, half_size, greet, 0)
    pl.semaphore_signal(barrier, inc=1, device_id={"seq": partner}, device_id_type=pl.DeviceIdType.MESH)
    for near in ((me + PLANE) % size, (me + size - PLANE) % size):
        pl.semaphore_signal(barrier, inc=1, device_id={"seq": near}, device_id_type=pl.DeviceIdType.MESH)
    pl.semaphore_wait(barrier, half_size + 2)

    def chunk_copies(chunk, peer, send, recv):
        return tuple(
            pltpu.make_async_remote_copy(
                src_ref=buf.at[chunk], dst_ref=buf.at[chunk],
                send_sem=send(which), recv_sem=recv(which),
                device_id={"seq": peer}, device_id_type=pl.DeviceIdType.MESH,
            )
            for which, buf in enumerate((ck, cv))
        )

    def up_copies(p):
        return chunk_copies(
            p * PLANE + me % PLANE, above, lambda w: up_sem.at[0, w, p], lambda w: up_sem.at[1, w, p]
        )

    def side_copies(p, y):
        return chunk_copies(
            p * PLANE + y * 2 + core, plane * PLANE + (1 - side) * 2 + core,
            lambda w: side_sem.at[0, w, p], lambda w: side_sem.at[1, w, p],
        )

    def core_copies(p, y, c):
        return chunk_copies(
            p * PLANE + y * 2 + c, plane * PLANE + side * 2 + (1 - core),
            lambda w: core_sem.at[0, w, p, y], lambda w: core_sem.at[1, w, p, y],
        )

    def start(copies):
        for copy in copies:
            copy.start()

    def arrive(copies):
        for copy in copies:
            copy.wait_recv()

    def left(copies):
        for copy in copies:
            copy.wait_send()

    def pass_on(p):
        @pl.when(plane < planes - 1)
        def _():
            start(up_copies(p))

        start(side_copies(p, side))
        start(core_copies(p, side, core))

    def pass_side(p):
        arrive(side_copies(p, 1 - side))
        start(core_copies(p, 1 - side, core))

    def query_copy():
        return pltpu.make_async_remote_copy(
            src_ref=q_ref, dst_ref=qp, send_sem=q_sem.at[0], recv_sem=q_sem.at[1],
            device_id={"seq": partner}, device_id_type=pl.DeviceIdType.MESH,
        )

    def self_copies(kind):
        asker = me if kind == 0 else partner
        return (
            pltpu.make_async_copy(sk_ref.at[asker], rk.at[kind, spot], self_sem.at[kind, 0]),
            pltpu.make_async_copy(sv_ref.at[asker], rv.at[kind, spot], self_sem.at[kind, 1]),
        )

    def slab_copies(kind, step):
        peer_spot = (spot + step) % half_size
        peer = mine * half_size + peer_spot
        asker = peer if kind == 0 else (1 - mine) * half_size + peer_spot
        return tuple(
            pltpu.make_async_remote_copy(
                src_ref=src.at[asker], dst_ref=dst.at[kind, spot],
                send_sem=send_sem.at[kind, which, step], recv_sem=recv_sem.at[kind, which, spot],
                device_id={"seq": peer}, device_id_type=pl.DeviceIdType.MESH,
            )
            for which, (src, dst) in enumerate(((sk_ref, rk), (sv_ref, rv)))
        )

    def slab_arrivals(kind, step):
        from_spot = (spot + step) % half_size
        return tuple(
            pltpu.make_async_remote_copy(
                src_ref=src.at[0], dst_ref=dst.at[kind, from_spot],
                send_sem=send_sem.at[kind, which, step], recv_sem=recv_sem.at[kind, which, from_spot],
                device_id={"seq": partner}, device_id_type=pl.DeviceIdType.MESH,
            )
            for which, (src, dst) in enumerate(((sk_ref, rk), (sv_ref, rv)))
        )

    def send_all(kind):
        def send(step, carry):
            for copy in slab_copies(kind, step):
                copy.start()
            return carry

        for copy in self_copies(kind):
            copy.start()
        lax.fori_loop(1, half_size, send, 0)

    def receive_all(kind):
        def receive(step, carry):
            for copy in slab_arrivals(kind, step):
                copy.wait_recv()
            return carry

        for copy in self_copies(kind):
            copy.wait()
        lax.fori_loop(1, half_size, receive, 0)

    def result_copy(g):
        part = pl.ds(pl.multiple_of(g * GROUP * HD, GROUP * HD), GROUP * HD)
        return pltpu.make_async_remote_copy(
            src_ref=po.at[:, part], dst_ref=ro.at[:, part],
            send_sem=res_sem.at[0, g], recv_sem=res_sem.at[1, g],
            device_id={"seq": partner}, device_id_type=pl.DeviceIdType.MESH,
        )

    def stats_copy():
        return pltpu.make_async_remote_copy(
            src_ref=ps, dst_ref=rs, send_sem=st_sem.at[0], recv_sem=st_sem.at[1],
            device_id={"seq": partner}, device_id_type=pl.DeviceIdType.MESH,
        )

    def head_state(kind, source, j):
        q = source[:, lanes_of(j)]
        kv = lanes_of(j // GROUP)
        state = fresh(rows)
        for t in range(half_size // SRCS):
            k = rk[kind, t * SRCS:(t + 1) * SRCS, :, kv].reshape(TILE, HD)
            v = rv[kind, t * SRCS:(t + 1) * SRCS, :, kv].reshape(TILE, HD)
            bias = None if bias_ref is None else bias_ref[kind, :, t * TILE:(t + 1) * TILE]
            state = tile_update(state, q, k, v, bias=bias)
        return state

    lane = lax.broadcasted_iota(jnp.int32, (rows, HD), 1)

    for copy in own_copies:
        copy.wait()
    pass_on(plane)

    def relay(t, carry):
        arrive(up_copies(plane - t))
        pass_on(plane - t)
        pass_side(plane - t + 1)
        return carry

    @pl.when(plane >= 1)
    def _():
        relay(1, 0)

    query_copy().start()
    send_all(1)
    send_all(0)
    query_copy().wait_recv()
    receive_all(1)

    stats = jnp.zeros((rows, HD), jnp.float32)
    for g in range(KVH):

        def serve(i, st, g=g):
            j = g * GROUP + i
            m, l, acc = head_state(1, qp, j)
            po[:, lanes_of(j)] = (acc / l).astype(jnp.bfloat16)
            st = jnp.where(lane == j, m, st)
            return jnp.where(lane == j + H, l, st)

        stats = lax.fori_loop(0, GROUP, serve, stats)
        if g == KVH - 1:
            ps[...] = stats
        else:
            if g >= 1:
                result_copy(g - 1).start()
            if g == 1:

                @pl.when(plane >= 2)
                def _():
                    relay(2, 0)

    lax.fori_loop(3, plane + 1, relay, 0)
    pass_side(0)
    result_copy(KVH - 2).start()

    def core_arrivals(t, carry):
        arrive(core_copies(t, side, 1 - core))
        arrive(core_copies(t, 1 - side, 1 - core))
        return carry

    lax.fori_loop(0, plane + 1, core_arrivals, 0)
    result_copy(KVH - 1).start()
    stats_copy().start()

    spots = me % PLANE * rows + lax.broadcasted_iota(jnp.int32, (rows, TILE), 0)
    allowed = lax.broadcasted_iota(jnp.int32, (rows, TILE), 1) <= spots

    def context_head(j, carry):
        q = q_ref[:, lanes_of(j)]
        kv = lanes_of(j // GROUP)

        def piece(t):
            at = pl.ds(t * PLANE, PLANE)
            return ck[at, :, kv].reshape(TILE, HD), cv[at, :, kv].reshape(TILE, HD)

        k, v = piece(plane)
        state = tile_update(fresh(rows), q, k, v, allowed=allowed)

        def step(t, state):
            k, v = piece(t)
            return tile_update(state, q, k, v)

        m, l, acc = lax.fori_loop(0, plane, step, state)
        out_ref[:, lanes_of(j)] = (acc / l).astype(jnp.bfloat16)
        return carry

    lax.fori_loop(0, H, context_head, 0)
    receive_all(0)

    def merge(j, state):
        m, l, acc = state
        there = rs[...]
        m_far = jnp.sum(jnp.where(lane == j, there, 0.0), axis=-1, keepdims=True)
        l_far = jnp.sum(jnp.where(lane == j + H, there, 0.0), axis=-1, keepdims=True)
        top = jnp.maximum(m, m_far)
        w = jnp.exp2(m - top)
        w_far = jnp.exp2(m_far - top) * l_far
        far = ro[:, lanes_of(j)].astype(jnp.float32)
        memory = ((acc * w + far * w_far) / (l * w + w_far)).astype(jnp.bfloat16).astype(jnp.float32)
        context = out_ref[:, lanes_of(j)].astype(jnp.float32)
        gate = gate_ref[j]
        out_ref[:, lanes_of(j)] = (gate * memory + (1.0 - gate) * context).astype(jnp.bfloat16)

    stats_copy().wait_recv()
    for g in range(KVH):
        result_copy(g).wait_recv()

        def finish(i, carry, g=g):
            j = g * GROUP + i
            merge(j, head_state(0, q_ref, j))
            return carry

        lax.fori_loop(0, GROUP, finish, 0)

    def drain_context(p, carry):
        @pl.when(plane < planes - 1)
        def _():
            left(up_copies(p))

        left(side_copies(p, side))
        left(core_copies(p, side, core))
        left(core_copies(p, 1 - side, core))
        return carry

    lax.fori_loop(0, plane + 1, drain_context, 0)
    query_copy().wait_send()
    for kind in (1, 0):

        def drain(step, carry, kind=kind):
            for copy in slab_copies(kind, step):
                copy.wait_send()
            return carry

        lax.fori_loop(1, half_size, drain, 0)
    for g in range(KVH):
        result_copy(g).wait_send()
    stats_copy().wait_send()


def attention_call(gate, queries, keys, values, send_keys, send_values, bias, size):
    rows = queries.shape[0]
    half_size = size // 2
    planes = size // PLANE
    operands = [gate, queries, keys, values, send_keys, send_values]
    specs = [
        pl.BlockSpec(memory_space=pltpu.SMEM),
        pl.BlockSpec(memory_space=pltpu.VMEM),
        pl.BlockSpec(memory_space=pl.ANY),
        pl.BlockSpec(memory_space=pl.ANY),
        pl.BlockSpec(memory_space=pl.ANY),
        pl.BlockSpec(memory_space=pl.ANY),
    ]
    if bias is not None:
        operands.append(bias)
        specs.append(pl.BlockSpec(memory_space=pltpu.VMEM))
    width = KVH * HD
    return pl.pallas_call(
        functools.partial(attention_kernel, size, bias is not None),
        out_shape=jax.ShapeDtypeStruct(queries.shape, jnp.bfloat16),
        in_specs=specs,
        out_specs=pl.BlockSpec(memory_space=pltpu.VMEM),
        scratch_shapes=[
            pltpu.VMEM(queries.shape, jnp.bfloat16),
            pltpu.VMEM((2, half_size, SLAB, width), jnp.bfloat16),
            pltpu.VMEM((2, half_size, SLAB, width), jnp.bfloat16),
            pltpu.VMEM(queries.shape, jnp.bfloat16),
            pltpu.VMEM((rows, HD), jnp.float32),
            pltpu.VMEM(queries.shape, jnp.bfloat16),
            pltpu.VMEM((rows, HD), jnp.float32),
            pltpu.VMEM((size, rows, width), jnp.bfloat16),
            pltpu.VMEM((size, rows, width), jnp.bfloat16),
            pltpu.SemaphoreType.DMA((2,)),
            pltpu.SemaphoreType.DMA((2, 2, half_size)),
            pltpu.SemaphoreType.DMA((2, 2, half_size)),
            pltpu.SemaphoreType.DMA((2, 2)),
            pltpu.SemaphoreType.DMA((2, KVH)),
            pltpu.SemaphoreType.DMA((2,)),
            pltpu.SemaphoreType.DMA((2,)),
            pltpu.SemaphoreType.DMA((2, 2, planes)),
            pltpu.SemaphoreType.DMA((2, 2, planes)),
            pltpu.SemaphoreType.DMA((2, 2, planes, 2)),
        ],
        compiler_params=pltpu.CompilerParams(
            collective_id=0, has_side_effects=True, vmem_limit_bytes=VMEM_LIMIT
        ),
        cost_estimate=pl.CostEstimate(
            flops=16 * 4096 * 256 * 512, bytes_accessed=200_000_000, transcendentals=16 * 4096 * 256
        ),
    )(*operands)


def on_device(
    queries, ctx_keys, ctx_values, store_keys, store_values, block_ids, block_slot, gate_logit
):
    size = lax.axis_size("seq")
    half_size = size // 2
    me = lax.axis_index("seq")
    local_count = store_keys.shape[0]
    my_slots = lookup_slots(block_ids.reshape(-1), block_slot)
    my_table = request_table(my_slots, size, CAP, local_count)
    wanted = lax.all_to_all(my_table, "seq", split_axis=0, concat_axis=0, tiled=True)
    rows_wanted = jnp.maximum(wanted, 0)
    width = KVH * HD
    send_keys = store_keys[rows_wanted].reshape(size, SLAB, width)
    send_values = store_values[rows_wanted].reshape(size, SLAB, width)
    bias = None
    if size * CAP != TOPM:
        tables = lax.all_gather(my_table, "seq", axis=0)
        half_start = me // half_size * half_size
        two = jnp.stack([tables[me], tables[(me + half_size) % size]])
        two = lax.dynamic_slice_in_dim(two, half_start, half_size, 1).reshape(2, half_size * CAP)
        bias = jnp.repeat(jnp.where(two < 0, NEG, 0.0).astype(jnp.float32), MROWS, axis=1)[:, None, :]
    gate = jax.nn.sigmoid(gate_logit)
    return attention_call(gate, queries, ctx_keys, ctx_values, send_keys, send_values, bias, size)


def solution(mesh):
    placed = (
        P(("groups", "seq"), None),
        P(("groups", "seq"), None),
        P(("groups", "seq"), None),
        P(("groups", "seq"), None, None),
        P(("groups", "seq"), None, None),
        P(("groups", "seq"), None),
        P("groups"),
        P(),
    )
    return jax.shard_map(
        on_device, mesh=mesh, in_specs=placed, out_specs=P(("groups", "seq"), None), check_vma=False
    )
```
